32 devices in a mesh: ctx: 8 (over z, y), tp: 4 (over x, core).
Axes of the slice: x: 2, y: 2, z: 4, core: 2. Of those that a mesh axis runs over, the one named last changes fastest.
Arguments:
- tokens: bfloat16 [4096, 5376], P(('ctx', 'tp')), may hold values from -8 to 8
- positions: int32 [4096], replicated, may hold values from 0 to 16383, as said below
- w_query: bfloat16 [5376, 2048], P('ctx', 'tp'), may hold values from -1 to 1
- key_matrix: bfloat16 [5376, 1024], P('ctx', 'tp'), may hold values from -1 to 1
- value_matrix: bfloat16 [5376, 1024], P('ctx', 'tp'), may hold values from -0.078125 to 0.078125
- w_out: bfloat16 [2048, 5376], P('tp', 'ctx'), may hold values from -0.125 to 0.125
- gain_in: float32 [5376], replicated, may hold values from 0.1 to 1.9
- gain_query: float32 [128], replicated, may hold values from 0.5 to 14
- gain_key: float32 [128], replicated, may hold values from 0.5 to 14
- gain_post: float32 [5376], replicated, may hold values from 0.1 to 1.9
Outputs:
- layer_out: bfloat16 [4096, 5376], P(('ctx', 'tp'))
The draws below stay inside these ranges and needn't reach their ends.
Inputs may be any that keep to these rules, and one draw needn't show every extreme that they name: (positions) rise strictly along the tokens, by 1 to 4 from one token to the next, and the last token stands at 16383.
All inputs are finite; a program needn't handle non-finite values.
Results may differ from the reference program's by a relative error of at most 0.013.
The reference program's roundings to bfloat16 on the way count: a program that leaves them out, or rounds other values in their place, can miss the bound.
Values may be sent and summed in bfloat16 or wider, within the bound.
A program may use at most 128 MiB of HBM per device.

```python
import jax
import jax.numpy as jnp
from jax import lax

MODEL_WIDTH = 5376
QUERY_HEAD_COUNT = 16
KEY_VALUE_HEADS = 8
HEAD_SIZE = 128
QS = 168
LOOKBACK_WINDOW = 1024
TOK_DEV = 512
TOKEN_COUNT = 4096


def draw_tokens(key, part):
    sampled_values = jax.random.normal(jax.random.fold_in(key, 1), (TOKEN_COUNT, MODEL_WIDTH), jnp.float32)
    return jnp.clip(sampled_values, -8.0, 8.0).astype(jnp.bfloat16)


def draw_positions(key, part):
    jumps = jax.random.randint(jax.random.fold_in(key, 12), (TOKEN_COUNT,), 0, 8) == 0
    extra = jax.random.randint(jax.random.fold_in(key, 13), (TOKEN_COUNT,), 1, 4)
    step_sizes = 1 + jnp.where(jumps, extra, 0)
    relative = jnp.cumsum(step_sizes) - step_sizes[0]
    last_pos = 4 * TOKEN_COUNT - 1
    return (last_pos - relative[-1] + relative).astype(jnp.int32)


def grouped_query(key):
    sampled_values = jax.random.normal(jax.random.fold_in(key, 101), (MODEL_WIDTH, QUERY_HEAD_COUNT * HEAD_SIZE), jnp.float32)
    return jnp.clip(sampled_values, -6.0, 6.0) * MODEL_WIDTH ** (-0.5)


def draw_w_query(key, part):
    return grouped_query(key).astype(jnp.bfloat16)


def draw_key_matrix(key, part):
    sampled_values = jax.random.normal(jax.random.fold_in(key, 103), (MODEL_WIDTH, KEY_VALUE_HEADS * HEAD_SIZE), jnp.float32)
    return (jnp.clip(sampled_values, -6.0, 6.0) * MODEL_WIDTH ** (-0.5)).astype(jnp.bfloat16)


def draw_gain_query(key, part):
    sampled_values = jax.random.uniform(jax.random.fold_in(key, 202), (HEAD_SIZE,), jnp.float32, 0.5, 2.0)
    return sampled_values


def draw_gain_key(key, part):
    sampled_values = jax.random.uniform(jax.random.fold_in(key, 203), (HEAD_SIZE,), jnp.float32, 0.5, 2.0)
    return sampled_values


def level_of(key, extent, shards, smallest, high):
    def one(axis_at, blocks):
        draws = jax.random.uniform(jax.random.fold_in(jax.random.fold_in(key, 6), axis_at), (blocks,), jnp.float32, smallest / len(shards), high / len(shards))
        return jnp.repeat(jnp.exp(draws), extent[axis_at] // blocks).reshape((-1,) + (1,) * (len(extent) - axis_at - 1))

    factor_of = one(*shards[0])
    for cut in shards[1:]:
        factor_of = factor_of * one(*cut)
    return factor_of


def bell_draw(rng, shape, scale, limit, pieces=(), kind=jnp.bfloat16):
    array = jax.random.normal(rng, shape, jnp.float32) * scale
    if len(pieces) > 0:
        array = level_of(rng, shape, pieces, -0.22, 0.18) * array
    return jnp.clip(array, min=-limit, max=limit).astype(kind)


def setup_inputs(seed: int = 0) -> dict:
    key_list = jax.random.split(jax.random.key(seed), 11)
    tokens = draw_tokens(jax.random.fold_in(key_list[10], 71), 0)
    positions = draw_positions(jax.random.fold_in(key_list[10], 71), 0)
    w_query = draw_w_query(jax.random.fold_in(key_list[10], 71), 0)
    key_matrix = draw_key_matrix(jax.random.fold_in(key_list[10], 71), 0)
    value_matrix = bell_draw(key_list[4], (MODEL_WIDTH, KEY_VALUE_HEADS * HEAD_SIZE), MODEL_WIDTH ** -0.5, 0.078125, ((0, 8), (1, 4)))
    w_out = bell_draw(key_list[5], (QUERY_HEAD_COUNT * HEAD_SIZE, MODEL_WIDTH), (QUERY_HEAD_COUNT * HEAD_SIZE) ** -0.5, 0.125, ((0, 4), (1, 8)))
    gain_in = jnp.clip(1.0 + 0.18 * jax.random.normal(key_list[6], (MODEL_WIDTH,), jnp.float32), 0.1, 1.9)
    gain_query = draw_gain_query(jax.random.fold_in(key_list[10], 71), 0)
    gain_key = draw_gain_key(jax.random.fold_in(key_list[10], 71), 0)
    gain_post = jnp.clip(1.0 + 0.18 * jax.random.normal(key_list[9], (MODEL_WIDTH,), jnp.float32), 0.1, 1.9)
    return {"tokens": tokens, "positions": positions, "w_query": w_query, "key_matrix": key_matrix, "value_matrix": value_matrix, "w_out": w_out, "gain_in": gain_in, "gain_query": gain_query, "gain_key": gain_key, "gain_post": gain_post}


EPSILON = 1e-06
ROPE_BASE = 10000.0

def row_norm(values, scales):
    mean_square = lax.optimization_barrier(jnp.mean(values * values, axis=-1, keepdims=True))
    return values * lax.rsqrt(mean_square + EPSILON) * scales

def rotate(head_rows, offsets):
    half_dim = head_rows.shape[-1] // 2
    frequency = ROPE_BASE ** (-(jnp.arange(half_dim, dtype=jnp.float32) * 2.0) / head_rows.shape[-1])
    angles = offsets.astype(jnp.float32)[:, None] * frequency[None, :]
    cosine = jnp.cos(angles)[:, None, :]
    sine_wave = jnp.sin(angles)[:, None, :]
    first_half = head_rows[..., :half_dim]
    second_half = head_rows[..., half_dim:]
    return jnp.concatenate([first_half * cosine - second_half * sine_wave, second_half * cosine + first_half * sine_wave], axis=-1)

def attend(query_matrix, projected_keys, projected_values, query_offsets, key_offsets, key_valid):
    scores = jnp.einsum('qkgd,skd->kgqs', query_matrix.astype(jnp.float32), projected_keys.astype(jnp.float32)) * QS ** (-0.5)
    position_gap = query_offsets[:, None] - key_offsets[None, :]
    allowed = key_valid[None, :] & (position_gap >= 0) & (position_gap < LOOKBACK_WINDOW)
    scores = jnp.where(allowed[None, None], scores, -1e+30)
    row_max = lax.optimization_barrier(jnp.max(scores, axis=-1, keepdims=True))
    weights = jnp.where(allowed[None, None], jnp.exp(scores - row_max), 0.0)
    totals = lax.optimization_barrier(jnp.sum(weights, axis=-1, keepdims=True))
    rounded = weights.astype(jnp.bfloat16)
    mixed = jnp.einsum('kgqs,skd->qkgd', rounded.astype(jnp.float32), projected_values.astype(jnp.float32))
    mixed = mixed / jnp.transpose(totals, (2, 0, 1, 3))
    return mixed.astype(jnp.bfloat16).reshape(query_matrix.shape[0], -1)

def reference(tokens, positions, w_query, key_matrix, value_matrix, w_out, gain_in, gain_query, gain_key, gain_post):
    normalized_rows = row_norm(tokens.astype(jnp.float32), gain_in).astype(jnp.bfloat16)
    offsets = positions - positions[0]
    query_raw = jnp.dot(normalized_rows, w_query, preferred_element_type=jnp.float32).reshape(TOKEN_COUNT, QUERY_HEAD_COUNT, HEAD_SIZE)
    unnormed_keys = jnp.dot(normalized_rows, key_matrix, preferred_element_type=jnp.float32).reshape(TOKEN_COUNT, KEY_VALUE_HEADS, HEAD_SIZE)
    projected_values = jnp.dot(normalized_rows, value_matrix, preferred_element_type=jnp.float32).astype(jnp.bfloat16).reshape(TOKEN_COUNT, KEY_VALUE_HEADS, HEAD_SIZE)
    query_matrix = rotate(row_norm(query_raw, gain_query), offsets).astype(jnp.bfloat16)
    projected_keys = rotate(row_norm(unnormed_keys, gain_key), offsets).astype(jnp.bfloat16)
    query_matrix = query_matrix.reshape(TOKEN_COUNT, KEY_VALUE_HEADS, QUERY_HEAD_COUNT // KEY_VALUE_HEADS, HEAD_SIZE)
    keys_with_padding = jnp.concatenate([jnp.zeros((LOOKBACK_WINDOW, KEY_VALUE_HEADS, HEAD_SIZE), jnp.bfloat16), projected_keys], axis=0)
    values_with_padding = jnp.concatenate([jnp.zeros((LOOKBACK_WINDOW, KEY_VALUE_HEADS, HEAD_SIZE), jnp.bfloat16), projected_values], axis=0)
    padded_offsets = jnp.concatenate([jnp.zeros((LOOKBACK_WINDOW,), jnp.int32), offsets.astype(jnp.int32)], axis=0)

    def one_block(block_index):
        block_begin = (block_index * TOK_DEV).astype(jnp.int32)
        query_block = lax.dynamic_slice_in_dim(query_matrix, block_begin, TOK_DEV, 0)
        query_offsets = lax.dynamic_slice_in_dim(offsets.astype(jnp.int32), block_begin, TOK_DEV, 0)
        key_block = lax.dynamic_slice_in_dim(keys_with_padding, block_begin, LOOKBACK_WINDOW + TOK_DEV, 0)
        value_block = lax.dynamic_slice_in_dim(values_with_padding, block_begin, LOOKBACK_WINDOW + TOK_DEV, 0)
        key_offsets = lax.dynamic_slice_in_dim(padded_offsets, block_begin, LOOKBACK_WINDOW + TOK_DEV, 0)
        key_valid = block_begin + jnp.arange(LOOKBACK_WINDOW + TOK_DEV, dtype=jnp.int32) >= LOOKBACK_WINDOW
        return attend(query_block, key_block, value_block, query_offsets, key_offsets, key_valid)
    blocks = lax.map(one_block, jnp.arange(TOKEN_COUNT // TOK_DEV, dtype=jnp.int32))
    attended = blocks.reshape(TOKEN_COUNT, QUERY_HEAD_COUNT * HEAD_SIZE)
    projected = jnp.dot(attended, w_out, preferred_element_type=jnp.float32)
    return (tokens.astype(jnp.float32) + row_norm(projected, gain_post)).astype(jnp.bfloat16)
```

```python
import jax
import jax.numpy as jnp
from jax import lax
from jax.experimental import pallas as pl
from jax.experimental.pallas import tpu as pltpu
from jax.sharding import PartitionSpec as P

HEAD_SIZE = 128
QS = 168
LOOKBACK_WINDOW = 1024


EPSILON = 1e-06
ROPE_BASE = 10000.0


def shifted(value, axis, steps):
    count = lax.axis_size(axis)
    leading, last = (max(0, -steps), min(count, count - steps))
    return lax.ppermute(value, axis, [(source, source + steps) for source in range(leading, last)])


def row_norm(values, scales):
    mean_square = jnp.mean(values * values, axis=-1, keepdims=True)
    return values * lax.rsqrt(mean_square + EPSILON) * scales


def rotate(head_rows, offsets):
    half_dim = head_rows.shape[-1] // 2
    frequency = ROPE_BASE ** (
        -(jnp.arange(half_dim, dtype=jnp.float32) * 2.0) / head_rows.shape[-1]
    )
    angles = offsets.astype(jnp.float32)[:, None] * frequency[None, :]
    cosine = jnp.cos(angles)[:, None, :]
    sine_wave = jnp.sin(angles)[:, None, :]
    first_half = head_rows[..., :half_dim]
    second_half = head_rows[..., half_dim:]
    return jnp.concatenate(
        [
            first_half * cosine - second_half * sine_wave,
            second_half * cosine + first_half * sine_wave,
        ],
        axis=-1,
    )


PIECES = 6
Z_SIZE = 4
MESH = pl.DeviceIdType.MESH


def gather_kernel(
    x_ref, q_ref, k_ref, v_ref, xg_ref, wg_ref,
    xs, ws, stage_sem, x_send, x_recv, y_send, y_recv, up_send, down_send, below_recv, above_recv,
):
    ctx = lax.axis_index("ctx")
    tp = lax.axis_index("tp")
    z, y = ctx // 2, ctx % 2
    y_other = 1 - y
    core_peer = tp + 1 - 2 * (tp % 2)
    x_peer = (tp + 2) % 4
    depth = q_ref.shape[0]
    piece = depth // PIECES
    tokens_own = x_ref.shape[0]
    q_width, k_width = q_ref.shape[1], k_ref.shape[1]
    y_id = (z * 2 + y_other, tp)
    up_id = (ctx + 2, tp)
    down_id = (ctx - 2, tp)
    core_id = (ctx, core_peer)
    x_id = (ctx, x_peer)

    barrier = pltpu.get_barrier_semaphore()

    def greet(target):
        pl.semaphore_signal(barrier, inc=1, device_id=target, device_id_type=MESH)

    greet(y_id)
    greet(core_id)
    greet(x_id)

    @pl.when(z < Z_SIZE - 1)
    def _():
        greet(up_id)

    @pl.when(z > 0)
    def _():
        greet(down_id)

    loads = [
        pltpu.make_async_copy(q_ref, ws.at[:, pl.ds(0, q_width)], stage_sem.at[0]),
        pltpu.make_async_copy(k_ref, ws.at[:, pl.ds(q_width, k_width)], stage_sem.at[1]),
        pltpu.make_async_copy(v_ref, ws.at[:, pl.ds(q_width + k_width, k_width)], stage_sem.at[2]),
        pltpu.make_async_copy(x_ref, xs, stage_sem.at[3]),
    ]
    for copy in loads:
        copy.start()
    for copy in loads:
        copy.wait()

    pl.semaphore_wait(barrier, 4 + ((z + 1) // 2) % 2)

    def rows(owner, part):
        return wg_ref.at[pl.ds(pl.multiple_of(owner * depth + part * piece, 16), piece)]

    def own_part(part):
        return ws.at[pl.ds(part * piece, piece)]

    def remote(source, target, send, recv, device):
        return pltpu.make_async_remote_copy(
            src_ref=source, dst_ref=target, send_sem=send, recv_sem=recv,
            device_id=device, device_id_type=MESH,
        )

    def place(plane, part):
        if part < PIECES:
            return rows(plane * 2 + y, part)
        return rows(plane * 2 + y_other, PIECES - 1)

    def y_copy(plane, part, own=False):
        target = rows(plane * 2 + y, part)
        if part == PIECES - 1:
            slot = Z_SIZE * (PIECES - 1)
        else:
            slot = plane * (PIECES - 1) + part
        return remote(
            own_part(part) if own else target, target, y_send.at[slot], y_recv.at[slot], y_id
        )

    def z_copy(plane, distance, part, upward):
        target = place(plane, part)
        source = own_part(part) if distance == 0 and part < PIECES else target
        slot = distance * (PIECES + 1) + part
        if upward:
            return remote(source, target, up_send.at[slot], below_recv.at[slot], up_id)
        return remote(source, target, down_send.at[slot], above_recv.at[slot], down_id)

    def arrived(plane, distance, part, from_below):
        target = place(plane, part)
        slot = (distance - 1) * (PIECES + 1) + part
        if from_below:
            return remote(target, target, up_send.at[slot], below_recv.at[slot], down_id)
        return remote(target, target, down_send.at[slot], above_recv.at[slot], up_id)

    def token_rows(owner):
        return xg_ref.at[pl.ds(pl.multiple_of(owner * tokens_own, 16), tokens_own)]

    def x_copy(owner, slot, device, own):
        target = token_rows(owner)
        return remote(xs if own else target, target, x_send.at[slot], x_recv.at[slot], device)

    def send_z(distance, part):
        @pl.when(z < Z_SIZE - 1)
        def _():
            z_copy(z, distance, part, True).start()

        @pl.when(z > 0)
        def _():
            z_copy(z, distance, part, False).start()

    y_copy(z, PIECES - 1, own=True).start()
    x_copy(tp, 0, x_id, True).start()
    x_copy(tp, 1, core_id, True).start()
    for part in range(PIECES - 1):
        send_z(0, part)
        y_copy(z, part, own=True).start()
    send_z(0, PIECES - 1)
    keep = [
        pltpu.make_async_copy(
            ws, wg_ref.at[pl.ds(pl.multiple_of(ctx * depth, 16), depth)], stage_sem.at[0]
        ),
        pltpu.make_async_copy(xs, token_rows(tp), stage_sem.at[3]),
    ]
    for copy in keep:
        copy.start()
    y_copy(z, PIECES - 1).wait_recv()
    send_z(0, PIECES)

    for distance in range(1, Z_SIZE):
        for part in range(PIECES + 1):
            @pl.when(z >= distance)
            def _():
                arrived(z - distance, distance, part, True).wait_recv()
                if distance < Z_SIZE - 1:
                    @pl.when(z < Z_SIZE - 1)
                    def _():
                        z_copy(z - distance, distance, part, True).start()
                if part < PIECES - 1:
                    y_copy(z - distance, part).start()

            @pl.when(z + distance < Z_SIZE)
            def _():
                arrived(z + distance, distance, part, False).wait_recv()
                if distance < Z_SIZE - 1:
                    @pl.when(z > 0)
                    def _():
                        z_copy(z + distance, distance, part, False).start()
                if part < PIECES - 1:
                    y_copy(z + distance, part).start()
        if distance == 1:
            x_copy(x_peer, 0, x_id, False).wait_recv()
            x_copy(x_peer, 2, core_id, False).start()

    x_copy(tp, 1, core_id, False).wait_recv()
    x_copy(x_peer, 2, core_id, False).wait_recv()
    for plane in range(Z_SIZE):
        for part in range(PIECES - 1):
            y_copy(plane, part).wait_recv()
    for plane in range(Z_SIZE):
        for part in range(PIECES - 1):
            y_copy(plane, part).wait_send()
    y_copy(z, PIECES - 1).wait_send()
    for slot in range(3):
        x_copy(tp, slot, core_id, True).wait_send()
    for distance in range(Z_SIZE - 1):
        for part in range(PIECES + 1):
            @pl.when((z < Z_SIZE - 1) & (z >= distance))
            def _():
                z_copy(z - distance, distance, part, True).wait_send()

            @pl.when((z > 0) & (z + distance < Z_SIZE))
            def _():
                z_copy(z + distance, distance, part, False).wait_send()
    for copy in keep:
        copy.wait()


def gather_inputs(normed, w_query, key_matrix, value_matrix):
    depth = w_query.shape[0]
    width = w_query.shape[1] + 2 * key_matrix.shape[1]
    tokens_own, model = normed.shape
    y_slots = Z_SIZE * (PIECES - 1) + 1
    z_slots = (Z_SIZE - 1) * (PIECES + 1)
    dma = pltpu.SemaphoreType.DMA
    return pl.pallas_call(
        gather_kernel,
        out_shape=(
            jax.ShapeDtypeStruct((4 * tokens_own, model), jnp.bfloat16),
            jax.ShapeDtypeStruct((2 * Z_SIZE * depth, width), jnp.bfloat16),
        ),
        in_specs=[pl.BlockSpec(memory_space=pl.ANY)] * 4,
        out_specs=(pl.BlockSpec(memory_space=pl.ANY),) * 2,
        scratch_shapes=[
            pltpu.VMEM((tokens_own, model), jnp.bfloat16),
            pltpu.VMEM((depth, width), jnp.bfloat16),
            dma((4,)), dma((3,)), dma((3,)), dma((y_slots,)), dma((y_slots,)),
            dma((z_slots,)), dma((z_slots,)), dma((z_slots,)), dma((z_slots,)),
        ],
        compiler_params=pltpu.CompilerParams(collective_id=0, has_side_effects=True),
        name="gather_inputs",
    )(normed, w_query, key_matrix, value_matrix)


def attend(query_matrix, projected_keys, projected_values, query_offsets, key_offsets, key_valid):
    scores = jnp.einsum(
        "qkgd,skd->kgqs", query_matrix, projected_keys, preferred_element_type=jnp.float32
    ) * QS ** (-0.5)
    position_gap = query_offsets[:, None] - key_offsets[None, :]
    allowed = key_valid[None, :] & (position_gap >= 0) & (position_gap < LOOKBACK_WINDOW)
    scores = jnp.where(allowed[None, None], scores, -1e30)
    row_max = jnp.max(scores, axis=-1, keepdims=True)
    weights = jnp.where(allowed[None, None], jnp.exp(scores - row_max), 0.0)
    totals = jnp.sum(weights, axis=-1, keepdims=True)
    rounded = weights.astype(jnp.bfloat16)
    mixed = jnp.einsum(
        "kgqs,skd->qkgd", rounded, projected_values, preferred_element_type=jnp.float32
    )
    mixed = mixed / jnp.transpose(totals, (2, 0, 1, 3))
    return mixed.astype(jnp.bfloat16).reshape(query_matrix.shape[0], -1)


def shards(
    tokens,
    positions,
    w_query,
    key_matrix,
    value_matrix,
    w_out,
    gain_in,
    gain_query,
    gain_key,
    gain_post,
):
    normed = row_norm(tokens.astype(jnp.float32), gain_in).astype(jnp.bfloat16)
    if lax.axis_size("ctx") == 2 * Z_SIZE and lax.axis_size("tp") == 4:
        normalized_rows, weights_in = gather_inputs(normed, w_query, key_matrix, value_matrix)
        normalized_rows, weights_in, w_out = lax.optimization_barrier(
            (normalized_rows, weights_in, w_out)
        )
    else:
        normalized_rows = lax.all_gather(normed, "tp", axis=0, tiled=True)
        weights_in = lax.all_gather(
            jnp.concatenate([w_query, key_matrix, value_matrix], axis=1), "ctx", axis=0, tiled=True
        )
    w_out_full = lax.all_gather(w_out, "ctx", axis=1, tiled=True)
    row_count = normalized_rows.shape[0]
    block_start = lax.axis_index("ctx") * row_count
    offsets_all = positions - positions[0]
    query_offsets = lax.dynamic_slice_in_dim(offsets_all, block_start, row_count, 0)
    raw = jnp.dot(normalized_rows, weights_in, preferred_element_type=jnp.float32)
    query_width, key_width = w_query.shape[1], key_matrix.shape[1]
    query_raw = raw[:, :query_width]
    unnormed_keys = raw[:, query_width : query_width + key_width]
    value_raw = raw[:, query_width + key_width :]
    key_heads = key_matrix.shape[1] // HEAD_SIZE
    projected_keys = rotate(
        row_norm(unnormed_keys.reshape(row_count, key_heads, HEAD_SIZE), gain_key), query_offsets
    ).astype(jnp.bfloat16)
    projected_values = value_raw.astype(jnp.bfloat16).reshape(row_count, key_heads, HEAD_SIZE)
    own_pair = jnp.stack([projected_keys, projected_values])
    window_blocks = LOOKBACK_WINDOW // row_count
    earlier = []
    carried = own_pair
    for relay_step in range(window_blocks):
        carried = shifted(carried, "ctx", 1)
        earlier.insert(0, carried)
    window_pair = jnp.concatenate(earlier + [own_pair], axis=1)
    query_heads = w_query.shape[1] // HEAD_SIZE
    query_matrix = rotate(
        row_norm(query_raw.reshape(row_count, query_heads, HEAD_SIZE), gain_query), query_offsets
    ).astype(jnp.bfloat16)
    query_matrix = query_matrix.reshape(row_count, key_heads, query_heads // key_heads, HEAD_SIZE)
    padded_offsets = jnp.concatenate(
        [jnp.zeros((LOOKBACK_WINDOW,), jnp.int32), offsets_all], axis=0
    )
    key_offsets = lax.dynamic_slice_in_dim(
        padded_offsets, block_start, LOOKBACK_WINDOW + row_count, 0
    )
    key_valid = (
        block_start + jnp.arange(LOOKBACK_WINDOW + row_count, dtype=jnp.int32) >= LOOKBACK_WINDOW
    )
    attended = attend(
        query_matrix, window_pair[0], window_pair[1], query_offsets, key_offsets, key_valid
    )
    projected = jnp.dot(
        attended,
        w_out_full,
        preferred_element_type=jnp.float32,
    )
    summed = lax.psum_scatter(
        projected.astype(jnp.bfloat16), "tp", scatter_dimension=0, tiled=True
    ).astype(jnp.float32)
    return (tokens.astype(jnp.float32) + row_norm(summed, gain_post)).astype(jnp.bfloat16)


def solution(mesh):
    in_specs = (
        P(("ctx", "tp"), None),
        P(),
        P("ctx", "tp"),
        P("ctx", "tp"),
        P("ctx", "tp"),
        P("tp", "ctx"),
        P(),
        P(),
        P(),
        P(),
    )
    out_specs = P(("ctx", "tp"), None)
    return jax.shard_map(shards, mesh=mesh, in_specs=in_specs, out_specs=out_specs, check_vma=False)
```

```python
import jax
import jax.numpy as jnp
from jax import lax
from jax.experimental import pallas as pl
from jax.experimental.pallas import tpu as pltpu
from jax.sharding import PartitionSpec as P

HEAD_SIZE = 128
QS = 168
LOOKBACK_WINDOW = 1024


EPSILON = 1e-06
ROPE_BASE = 10000.0


def shifted(value, axis, steps):
    count = lax.axis_size(axis)
    leading, last = (max(0, -steps), min(count, count - steps))
    return lax.ppermute(value, axis, [(source, source + steps) for source in range(leading, last)])


def row_norm(values, scales):
    mean_square = jnp.mean(values * values, axis=-1, keepdims=True)
    return values * lax.rsqrt(mean_square + EPSILON) * scales


def rotate(head_rows, offsets):
    half_dim = head_rows.shape[-1] // 2
    frequency = ROPE_BASE ** (
        -(jnp.arange(half_dim, dtype=jnp.float32) * 2.0) / head_rows.shape[-1]
    )
    angles = offsets.astype(jnp.float32)[:, None] * frequency[None, :]
    cosine = jnp.cos(angles)[:, None, :]
    sine_wave = jnp.sin(angles)[:, None, :]
    first_half = head_rows[..., :half_dim]
    second_half = head_rows[..., half_dim:]
    return jnp.concatenate(
        [
            first_half * cosine - second_half * sine_wave,
            second_half * cosine + first_half * sine_wave,
        ],
        axis=-1,
    )


Z_SIZE = 4
TILE = 16
CUTS = (0, 11, 23, 35, 42)
PIECES = len(CUTS) - 1
ROW_STEP = 336
MESH = pl.DeviceIdType.MESH


def remote(source, target, send, recv, device):
    return pltpu.make_async_remote_copy(
        src_ref=source, dst_ref=target, send_sem=send, recv_sem=recv,
        device_id=device, device_id_type=MESH,
    )


class Places:
    def __init__(self):
        self.ctx = lax.axis_index("ctx")
        self.tp = lax.axis_index("tp")
        self.z, self.y = self.ctx // 2, self.ctx % 2
        self.y_other = 1 - self.y
        self.x_peer = (self.tp + 2) % 4
        self.y_id = (self.z * 2 + self.y_other, self.tp)
        self.up_id = (self.ctx + 2, self.tp)
        self.down_id = (self.ctx - 2, self.tp)
        self.core_id = (self.ctx, self.tp + 1 - 2 * (self.tp % 2))
        self.x_id = (self.ctx, self.x_peer)

    def greet(self):
        barrier = pltpu.get_barrier_semaphore()

        def signal(target):
            pl.semaphore_signal(barrier, inc=1, device_id=target, device_id_type=MESH)

        signal(self.y_id)
        signal(self.core_id)
        signal(self.x_id)

        @pl.when(self.z < Z_SIZE - 1)
        def _():
            signal(self.up_id)

        @pl.when(self.z > 0)
        def _():
            signal(self.down_id)

    def meet(self):
        z = self.z
        pl.semaphore_wait(pltpu.get_barrier_semaphore(), 4 + ((z + 1) // 2) % 2)


class Gather:
    def __init__(self, places, own, whole, depth, sems):
        self.at, self.own, self.whole, self.depth = places, own, whole, depth
        self.y_send, self.y_recv, self.up_send, self.down_send, self.below, self.above = sems

    def rows(self, owner, part):
        start, stop = CUTS[part] * TILE, CUTS[part + 1] * TILE
        return self.whole.at[
            pl.ds(pl.multiple_of(owner * self.depth + start, TILE), stop - start)
        ]

    def own_part(self, part):
        return self.own(CUTS[part] * TILE, (CUTS[part + 1] - CUTS[part]) * TILE)

    def place(self, plane, part):
        if part < PIECES:
            return self.rows(plane * 2 + self.at.y, part)
        return self.rows(plane * 2 + self.at.y_other, PIECES - 1)

    def y_copy(self, plane, part, own=False):
        target = self.rows(plane * 2 + self.at.y, part)
        slot = Z_SIZE * (PIECES - 1) if part == PIECES - 1 else plane * (PIECES - 1) + part
        source = self.own_part(part) if own else target
        return remote(source, target, self.y_send.at[slot], self.y_recv.at[slot], self.at.y_id)

    def z_copy(self, plane, distance, part, upward):
        target = self.place(plane, part)
        source = self.own_part(part) if distance == 0 and part < PIECES else target
        slot = distance * (PIECES + 1) + part
        if upward:
            return remote(
                source, target, self.up_send.at[slot], self.below.at[slot], self.at.up_id
            )
        return remote(
            source, target, self.down_send.at[slot], self.above.at[slot], self.at.down_id
        )

    def send_z(self, part):
        z = self.at.z

        @pl.when(z < Z_SIZE - 1)
        def _():
            self.z_copy(z, 0, part, True).start()

        @pl.when(z > 0)
        def _():
            self.z_copy(z, 0, part, False).start()

    def start(self):
        z = self.at.z
        self.y_copy(z, PIECES - 1, own=True).start()
        for part in range(PIECES - 1):
            self.send_z(part)
            self.y_copy(z, part, own=True).start()
        self.send_z(PIECES - 1)

    def cross(self):
        self.y_copy(self.at.z, PIECES - 1).wait_recv()
        self.send_z(PIECES)

    def relay(self, distance, part):
        z = self.at.z

        @pl.when(z >= distance)
        def _():
            self.z_copy(z - distance, distance - 1, part, True).wait_recv()
            if distance < Z_SIZE - 1:
                @pl.when(z < Z_SIZE - 1)
                def _():
                    self.z_copy(z - distance, distance, part, True).start()
            if part < PIECES - 1:
                self.y_copy(z - distance, part).start()

        @pl.when(z + distance < Z_SIZE)
        def _():
            self.z_copy(z + distance, distance - 1, part, False).wait_recv()
            if distance < Z_SIZE - 1:
                @pl.when(z > 0)
                def _():
                    self.z_copy(z + distance, distance, part, False).start()
            if part < PIECES - 1:
                self.y_copy(z + distance, part).start()

    def wait_plane(self, plane):
        for part in range(PIECES - 1):
            self.y_copy(plane, part).wait_recv()

    def drain(self):
        z = self.at.z
        for plane in range(Z_SIZE):
            for part in range(PIECES - 1):
                self.y_copy(plane, part).wait_send()
        self.y_copy(z, PIECES - 1).wait_send()
        for distance in range(Z_SIZE - 1):
            for part in range(PIECES + 1):
                @pl.when((z < Z_SIZE - 1) & (z >= distance))
                def _():
                    self.z_copy(z - distance, distance, part, True).wait_send()

                @pl.when((z > 0) & (z + distance < Z_SIZE))
                def _():
                    self.z_copy(z + distance, distance, part, False).wait_send()


def gather_semaphores():
    y_slots = Z_SIZE * (PIECES - 1) + 1
    z_slots = (Z_SIZE - 1) * (PIECES + 1)
    return [pltpu.SemaphoreType.DMA((n,)) for n in (y_slots, y_slots) + (z_slots,) * 4]


def gather_kernel(
    x_ref, q_ref, k_ref, v_ref, xg_ref, wg_ref, xs, ws, stage_sem, x_send, x_recv, *sems
):
    at = Places()
    depth, tokens_own = q_ref.shape[0], x_ref.shape[0]
    q_width, k_width = q_ref.shape[1], k_ref.shape[1]
    at.greet()
    loads = [
        pltpu.make_async_copy(q_ref, ws.at[:, pl.ds(0, q_width)], stage_sem.at[0]),
        pltpu.make_async_copy(k_ref, ws.at[:, pl.ds(q_width, k_width)], stage_sem.at[1]),
        pltpu.make_async_copy(v_ref, ws.at[:, pl.ds(q_width + k_width, k_width)], stage_sem.at[2]),
        pltpu.make_async_copy(x_ref, xs, stage_sem.at[3]),
    ]
    for copy in loads:
        copy.start()
    for copy in loads:
        copy.wait()
    at.meet()
    gather = Gather(at, lambda begin, size: ws.at[pl.ds(begin, size)], wg_ref, depth, sems)

    def token_rows(owner):
        return xg_ref.at[pl.ds(pl.multiple_of(owner * tokens_own, TILE), tokens_own)]

    def x_copy(owner, slot, device, own):
        target = token_rows(owner)
        return remote(xs if own else target, target, x_send.at[slot], x_recv.at[slot], device)

    x_copy(at.tp, 0, at.x_id, True).start()
    x_copy(at.tp, 1, at.core_id, True).start()
    gather.start()
    keep = [
        pltpu.make_async_copy(
            ws, wg_ref.at[pl.ds(pl.multiple_of(at.ctx * depth, TILE), depth)], stage_sem.at[0]
        ),
        pltpu.make_async_copy(xs, token_rows(at.tp), stage_sem.at[3]),
    ]
    for copy in keep:
        copy.start()
    gather.cross()
    for distance in range(1, Z_SIZE):
        for part in range(PIECES + 1):
            gather.relay(distance, part)
        if distance == 1:
            x_copy(at.x_peer, 0, at.x_id, False).wait_recv()
            x_copy(at.x_peer, 2, at.core_id, False).start()
    x_copy(at.tp, 1, at.core_id, False).wait_recv()
    x_copy(at.x_peer, 2, at.core_id, False).wait_recv()
    for plane in range(Z_SIZE):
        gather.wait_plane(plane)
    gather.drain()
    for slot in range(3):
        x_copy(at.tp, slot, at.core_id, True).wait_send()
    for copy in keep:
        copy.wait()


def gather_inputs(normed, w_query, key_matrix, value_matrix):
    depth = w_query.shape[0]
    width = w_query.shape[1] + 2 * key_matrix.shape[1]
    tokens_own, model = normed.shape
    dma = pltpu.SemaphoreType.DMA
    return pl.pallas_call(
        gather_kernel,
        out_shape=(
            jax.ShapeDtypeStruct((4 * tokens_own, model), jnp.bfloat16),
            jax.ShapeDtypeStruct((2 * Z_SIZE * depth, width), jnp.bfloat16),
        ),
        in_specs=[pl.BlockSpec(memory_space=pl.ANY)] * 4,
        out_specs=(pl.BlockSpec(memory_space=pl.ANY),) * 2,
        scratch_shapes=[
            pltpu.VMEM((tokens_own, model), jnp.bfloat16),
            pltpu.VMEM((depth, width), jnp.bfloat16),
            dma((4,)), dma((3,)), dma((3,)), *gather_semaphores(),
        ],
        compiler_params=pltpu.CompilerParams(collective_id=0, has_side_effects=True),
        name="gather_inputs",
    )(normed, w_query, key_matrix, value_matrix)


def project_kernel(
    w_ref, mine_ref, peer_ref, out_ref,
    whole, kept, sent_core, got_core, sent_x, got_x,
    stage_sem, core_send, core_recv, x_send, x_recv, *sems,
):
    at = Places()
    depth = w_ref.shape[0]
    tokens_own = out_ref.shape[1]
    plane_rows = 2 * depth
    z = at.z
    at.greet()

    def own_rows(begin, size):
        return whole.at[pl.ds(pl.multiple_of(at.ctx * depth + begin, TILE), size)]

    load = pltpu.make_async_copy(w_ref, own_rows(0, depth), stage_sem)
    load.start()
    load.wait()
    at.meet()
    gather = Gather(at, own_rows, whole, depth, sems)
    planes = [z, z + 1 - 2 * (z % 2), (z + 2) % 4, 3 - z]
    x_mine = at.tp // 2
    mine_columns = pl.ds(pl.multiple_of(x_mine * tokens_own, 128), tokens_own)
    other_columns = pl.ds(pl.multiple_of((1 - x_mine) * tokens_own, 128), tokens_own)

    def core_copy(step):
        return remote(
            sent_core.at[step], got_core.at[step], core_send.at[step], core_recv.at[step],
            at.core_id,
        )

    def x_copy(step):
        return remote(
            sent_x.at[step], got_x.at[step], x_send.at[step], x_recv.at[step], at.x_id
        )

    def product(rows, tokens):
        return lax.dot_general(
            rows, tokens, (((1,), (1,)), ((), ())), preferred_element_type=jnp.float32
        )

    def project(step):
        first = planes[step] * plane_rows

        @pl.loop(0, plane_rows // ROW_STEP)
        def _(block):
            rows = whole[pl.ds(pl.multiple_of(first + block * ROW_STEP, TILE), ROW_STEP), :]
            here = pl.ds(pl.multiple_of(block * ROW_STEP, TILE), ROW_STEP)
            sent_core[step, here, :] = product(rows, peer_ref[...]).astype(jnp.bfloat16)
            kept[step, here, :] = product(rows, mine_ref[...])

        core_copy(step).start()

    def pass_on(step):
        core_copy(step).wait_recv()

        @pl.loop(0, plane_rows // ROW_STEP)
        def _(block):
            here = pl.ds(pl.multiple_of(block * ROW_STEP, TILE), ROW_STEP)
            total = kept[step, here, other_columns] + got_core[step, here, other_columns].astype(
                jnp.float32
            )
            sent_x[step, here, :] = total.astype(jnp.bfloat16)

        x_copy(step).start()

    def finish(step):
        x_copy(step).wait_recv()
        first = planes[step] * plane_rows

        @pl.loop(0, plane_rows // ROW_STEP)
        def _(block):
            here = pl.ds(pl.multiple_of(block * ROW_STEP, TILE), ROW_STEP)
            there = pl.ds(pl.multiple_of(first + block * ROW_STEP, TILE), ROW_STEP)
            out_ref[there, :] = (
                kept[step, here, mine_columns]
                + got_core[step, here, mine_columns].astype(jnp.float32)
                + got_x[step, here, :].astype(jnp.float32)
            )

    gather.start()
    gather.cross()
    gather.wait_plane(z)
    project(0)
    for distance in range(1, Z_SIZE):
        for part in range(PIECES + 1):
            gather.relay(distance, part)
            if part == 1:
                pass_on(distance - 1)
        gather.wait_plane(planes[distance])
        project(distance)
    pass_on(Z_SIZE - 1)
    for step in range(Z_SIZE):
        finish(step)
    gather.drain()
    for step in range(Z_SIZE):
        core_copy(step).wait_send()
        x_copy(step).wait_send()


def project_out(w_rows, mine, peer):
    depth, heads = w_rows.shape
    tokens_own = mine.shape[0] // 2
    plane_rows = 2 * depth
    bf16, dma = jnp.bfloat16, pltpu.SemaphoreType.DMA
    vmem = pl.BlockSpec(memory_space=pltpu.VMEM)
    return pl.pallas_call(
        project_kernel,
        out_shape=jax.ShapeDtypeStruct((Z_SIZE * plane_rows, tokens_own), jnp.float32),
        in_specs=[pl.BlockSpec(memory_space=pl.ANY), vmem, vmem],
        out_specs=vmem,
        scratch_shapes=[
            pltpu.VMEM((Z_SIZE * plane_rows, heads), bf16),
            pltpu.VMEM((Z_SIZE, plane_rows, 2 * tokens_own), jnp.float32),
            pltpu.VMEM((Z_SIZE, plane_rows, 2 * tokens_own), bf16),
            pltpu.VMEM((Z_SIZE, plane_rows, 2 * tokens_own), bf16),
            pltpu.VMEM((Z_SIZE, plane_rows, tokens_own), bf16),
            pltpu.VMEM((Z_SIZE, plane_rows, tokens_own), bf16),
            dma, dma((Z_SIZE,)), dma((Z_SIZE,)), dma((Z_SIZE,)), dma((Z_SIZE,)),
            *gather_semaphores(),
        ],
        compiler_params=pltpu.CompilerParams(collective_id=1, has_side_effects=True),
        name="project_out",
    )(w_rows, mine, peer)


def attend(query_matrix, projected_keys, projected_values, query_offsets, key_offsets, key_valid):
    scores = jnp.einsum(
        "qkgd,skd->kgqs", query_matrix, projected_keys, preferred_element_type=jnp.float32
    ) * QS ** (-0.5)
    position_gap = query_offsets[:, None] - key_offsets[None, :]
    allowed = key_valid[None, :] & (position_gap >= 0) & (position_gap < LOOKBACK_WINDOW)
    scores = jnp.where(allowed[None, None], scores, -1e30)
    row_max = jnp.max(scores, axis=-1, keepdims=True)
    weights = jnp.where(allowed[None, None], jnp.exp(scores - row_max), 0.0)
    totals = jnp.sum(weights, axis=-1, keepdims=True)
    rounded = weights.astype(jnp.bfloat16)
    mixed = jnp.einsum(
        "kgqs,skd->qkgd", rounded, projected_values, preferred_element_type=jnp.float32
    )
    mixed = mixed / jnp.transpose(totals, (2, 0, 1, 3))
    return mixed.astype(jnp.bfloat16).reshape(query_matrix.shape[0], -1)


def shards(
    tokens,
    positions,
    w_query,
    key_matrix,
    value_matrix,
    w_out,
    gain_in,
    gain_query,
    gain_key,
    gain_post,
):
    normed = row_norm(tokens.astype(jnp.float32), gain_in).astype(jnp.bfloat16)
    kernels = lax.axis_size("ctx") == 2 * Z_SIZE and lax.axis_size("tp") == 4
    if kernels:
        normalized_rows, weights_in = gather_inputs(normed, w_query, key_matrix, value_matrix)
    else:
        normalized_rows = lax.all_gather(normed, "tp", axis=0, tiled=True)
        weights_in = lax.all_gather(
            jnp.concatenate([w_query, key_matrix, value_matrix], axis=1), "ctx", axis=0, tiled=True
        )
    row_count = normalized_rows.shape[0]
    block_start = lax.axis_index("ctx") * row_count
    offsets_all = positions - positions[0]
    query_offsets = lax.dynamic_slice_in_dim(offsets_all, block_start, row_count, 0)
    query_width, key_width = w_query.shape[1], key_matrix.shape[1]

    def add_rows(weights):
        return jnp.dot(normalized_rows, weights, preferred_element_type=jnp.float32)

    key_value_raw = add_rows(weights_in[:, query_width:])
    query_raw = add_rows(weights_in[:, :query_width])
    unnormed_keys = key_value_raw[:, :key_width]
    value_raw = key_value_raw[:, key_width:]
    key_heads = key_matrix.shape[1] // HEAD_SIZE
    projected_keys = rotate(
        row_norm(unnormed_keys.reshape(row_count, key_heads, HEAD_SIZE), gain_key), query_offsets
    ).astype(jnp.bfloat16)
    projected_values = value_raw.astype(jnp.bfloat16).reshape(row_count, key_heads, HEAD_SIZE)
    own_pair = jnp.stack([projected_keys, projected_values])
    window_blocks = LOOKBACK_WINDOW // row_count
    earlier = [shifted(own_pair, "ctx", steps) for steps in range(window_blocks, 0, -1)]
    window_pair = jnp.concatenate(earlier + [own_pair], axis=1)
    query_heads = w_query.shape[1] // HEAD_SIZE
    query_matrix = rotate(
        row_norm(query_raw.reshape(row_count, query_heads, HEAD_SIZE), gain_query), query_offsets
    ).astype(jnp.bfloat16)
    query_matrix = query_matrix.reshape(row_count, key_heads, query_heads // key_heads, HEAD_SIZE)
    padded_offsets = jnp.concatenate(
        [jnp.zeros((LOOKBACK_WINDOW,), jnp.int32), offsets_all], axis=0
    )
    key_offsets = lax.dynamic_slice_in_dim(
        padded_offsets, block_start, LOOKBACK_WINDOW + row_count, 0
    )
    key_valid = (
        block_start + jnp.arange(LOOKBACK_WINDOW + row_count, dtype=jnp.int32) >= LOOKBACK_WINDOW
    )
    attended = attend(
        query_matrix, window_pair[0], window_pair[1], query_offsets, key_offsets, key_valid
    )
    if kernels:
        by_core = attended.reshape(2, 2, row_count // 4, attended.shape[1])
        core = lax.axis_index("tp") % 2
        mine = lax.dynamic_index_in_dim(by_core, core, 1, keepdims=False)
        peer = lax.dynamic_index_in_dim(by_core, 1 - core, 1, keepdims=False)
        flat = (row_count // 2, attended.shape[1])
        summed = project_out(w_out.T, mine.reshape(flat), peer.reshape(flat)).T
    else:
        projected = jnp.dot(
            attended,
            lax.all_gather(w_out, "ctx", axis=1, tiled=True),
            preferred_element_type=jnp.float32,
        )
        summed = lax.psum_scatter(
            projected.astype(jnp.bfloat16), "tp", scatter_dimension=0, tiled=True
        ).astype(jnp.float32)
    return (tokens.astype(jnp.float32) + row_norm(summed, gain_post)).astype(jnp.bfloat16)


def solution(mesh):
    in_specs = (
        P(("ctx", "tp"), None),
        P(),
        P("ctx", "tp"),
        P("ctx", "tp"),
        P("ctx", "tp"),
        P("tp", "ctx"),
        P(),
        P(),
        P(),
        P(),
    )
    out_specs = P(("ctx", "tp"), None)
    return jax.shard_map(shards, mesh=mesh, in_specs=in_specs, out_specs=out_specs, check_vma=False)
```
